1024 devices in a mesh: node: 64 (over z, core), local: 4 (over y), tp: 4 (over x).
Axes of the slice: x: 4, y: 4, z: 32, core: 2. Of those that a mesh axis runs over, the one named last changes fastest.
Arguments:
- tokens: bfloat16 [8192, 2048], P(('node', 'local'), 'tp'), may hold values from -6 to 6
- grad_out: bfloat16 [8192, 2048], P(('node', 'local'), 'tp'), may hold values from -6 to 6
- routes: int32 [8192, 8], P(('node', 'local')), may hold values from 0 to 127, all different within a row; in each aligned block of 32 rows (0 to 31, 32 to 63, ...) at most 3 rows name the same one
- route_weight: float32 [8192, 8], P(('node', 'local')), may hold values from 0.05 to 0.5
- w_gate: bfloat16 [256, 2048, 384], P(('node', 'local'), 'tp'), may hold values from -0.125 to 0.125
- w_up: bfloat16 [256, 2048, 384], P(('node', 'local'), 'tp'), may hold values from -0.125 to 0.125
- w_down: bfloat16 [256, 384, 2048], P(('node', 'local'), None, 'tp'), may hold values from -0.21875 to 0.21875
Outputs:
- mixed: bfloat16 [8192, 2048], P(('node', 'local'), 'tp')
- grad_tokens: bfloat16 [8192, 2048], P(('node', 'local'), 'tp')
- grad_gate: bfloat16 [256, 2048, 384], P(('node', 'local'), 'tp')
- grad_up: bfloat16 [256, 2048, 384], P(('node', 'local'), 'tp')
- grad_down: bfloat16 [256, 384, 2048], P(('node', 'local'), None, 'tp')
The draws below stay inside these ranges and needn't reach their ends.
Inputs may be any that keep to these rules, and one draw needn't show every extreme that they name: `routes`: each row names 8 different experts; within each aligned block of 32 rows (the tokens of one index of node and local) no expert is named more than 3 times, a bound that some block reaches.
All inputs are finite; a program needn't handle non-finite values.
Results may differ from the reference program's by a relative error of at most 0.02.
Values may be sent and summed in bfloat16 or wider, within the bound.
A program may use at most 32 MiB of HBM per device.

```python
import math
import jax
import jax.numpy as jnp
import numpy as np
from jax import lax

D = 2048
FF = 768
TOPK = 8
TOK_DEV = 32
EXPERTS = 128
CAP = 3
TOKENS = 8192
HALF = 384
D_DEV = 512
N_NODE = 64
N_LOCAL = 4
N_TP = 4


def shard_levels(rng, extent, cuts, least, largest):
    level, own = 1.0, jax.random.fold_in(rng, 6)
    for dim, blocks in cuts:
        steps = jnp.exp(jax.random.uniform(jax.random.fold_in(own, dim), (blocks,), jnp.float32, least / len(cuts), largest / len(cuts)))
        level = level * jnp.repeat(steps, extent[dim] // blocks).reshape([-1 if axis == dim else 1 for axis in range(len(extent))])
    return level


def assign_block(key, own, number, rows, count, top, reach, lean):
    order = jax.random.permutation(key, count)
    packed, usual = load_shares(count, rows * top, reach, lean, True), load_shares(count, rows * top, reach, lean, False)
    places = jnp.arange(count)

    def named(sizes, turn):
        used = int((sizes > 0).sum())
        fixed = max(1, used // 4)
        passed = fixed + (places - fixed + turn * (used - fixed)) % max(1, count - fixed)
        return jnp.zeros((count,), jnp.int32).at[order[jnp.where(places < fixed, places, passed)]].set(jnp.asarray(sizes, jnp.int32))

    sizes = jnp.where(number % 4 == 0, named(packed, number // 4), named(usual, number - number // 4 - 1))
    mixed = jax.random.permutation(jax.random.fold_in(own, 3), count)
    donor, taker = mixed[0:count // 2 * 2:2], mixed[1:count // 2 * 2:2]
    room = jnp.minimum(sizes[donor] - 1, reach - sizes[taker]) // 2
    room = jnp.where((donor == order[0]) | (taker == order[0]) | (sizes[taker] == 0), 0, jnp.maximum(room, 0))
    passed = jax.random.randint(jax.random.fold_in(own, 4), (count // 2,), 0, 1 << 20) % (room + 1)
    sizes = sizes.at[donor].add(-passed).at[taker].add(passed)
    labels = jnp.searchsorted(jnp.cumsum(sizes), jnp.arange(rows * top), side="right").astype(jnp.int32)
    table = labels.reshape(top, rows).T
    table = table[jax.random.permutation(jax.random.fold_in(own, 1), rows)]
    turn = jax.random.randint(jax.random.fold_in(own, 2), (rows, 1), 0, top)
    return jnp.take_along_axis(table, (jnp.arange(top)[None, :] + turn) % top, axis=1)


def load_shares(count, total, bound, lean, full):
    portions = [(1 << 20) // math.isqrt(standing ** lean) + 1 for standing in range(1, count + 1)]
    largest = bound if full else min(bound, max(-(-total // count), total * portions[0] // sum(portions)))
    least = 1 if total - largest >= count - 1 else 0
    given, surplus = [largest] + [least] * (count - 1), total - largest - least * (count - 1)
    while surplus > 0:
        movable = [i for i in range(1, count) if given[i] < largest] or [i for i in range(1, count) if given[i] < bound]
        whole, remaining = sum([portions[i] for i in movable]), surplus
        for i in movable:
            extra = min(bound - given[i], max(1, remaining * portions[i] // whole), surplus)
            given[i] = given[i] + extra
            surplus = surplus - extra
    return np.array(given)


def centred(rng, extent, spread, reach, shards=(), held_as=jnp.bfloat16):
    drawn = jax.random.normal(rng, extent, jnp.float32) * spread
    if len(shards) > 0:
        drawn = shard_levels(rng, extent, shards, -0.22, 0.18) * drawn
    return jnp.clip(drawn, min=-reach, max=reach).astype(held_as)


def setup_inputs(seed: int = 0) -> dict:
    splits = jax.random.split(jax.random.key(seed), 8)
    tokens = centred(splits[0], (TOKENS, D), 1.0, 6.0, ((0, 256), (1, 4)))
    grad_out = centred(splits[1], (TOKENS, D), 1.0, 6.0, ((0, 256), (1, 4)))
    routes_keys = jax.random.split(jax.random.fold_in(splits[2], 1), TOKENS // TOK_DEV)
    routes_turns = jax.random.permutation(jax.random.fold_in(splits[2], 3), TOKENS // TOK_DEV)
    routes = jax.vmap(lambda own, number: assign_block(jax.random.fold_in(splits[2], 2), own, number, TOK_DEV, EXPERTS, TOPK, CAP, 2))(routes_keys, routes_turns).reshape((TOKENS, TOPK))
    route_weight = jnp.clip(jnp.exp(math.log(0.5) - 2.3025851 * jax.random.uniform(splits[3], (TOKENS, TOPK), jnp.float32) ** shard_levels(splits[3], (TOKENS, TOPK), ((0, 256),), -0.2, 0.2)), 0.05, 0.5)
    w_gate = centred(splits[4], (2 * EXPERTS, D, HALF), D ** -0.5, 0.125, ((0, 256), (1, 4)))
    w_up = centred(splits[5], (2 * EXPERTS, D, HALF), D ** -0.5, 0.125, ((0, 256), (1, 4)))
    w_down = centred(splits[6], (2 * EXPERTS, HALF, D), FF ** -0.5, 0.21875, ((0, 256), (2, 4)))
    return dict(tokens=tokens, grad_out=grad_out, routes=routes, route_weight=route_weight, w_gate=w_gate, w_up=w_up, w_down=w_down)


def slot_table(route_rows, experts, capacity):
    flat = route_rows.reshape(-1)
    count = flat.shape[0]
    onehot = (flat[:, None] == jnp.arange(experts, dtype=jnp.int32)[None, :]).astype(jnp.float32)
    lower = (jnp.arange(count)[:, None] > jnp.arange(count)[None, :]).astype(jnp.float32)
    before = jnp.dot(lower, onehot, precision=lax.Precision.HIGHEST)
    ranking = jnp.sum(before * onehot, axis=1).astype(jnp.int32)
    position = flat * capacity + ranking
    return (position[None, :] == jnp.arange(experts * capacity, dtype=jnp.int32)[:, None]).astype(jnp.float32)


def piece_sum(parts):
    rounded = lax.optimization_barrier(parts.astype(jnp.bfloat16))
    return jnp.sum(rounded.astype(jnp.float32), axis=0)


def half_pass(x_rows, g_rows, weight_g, weight_u, weight_d):
    hi = lax.Precision.HIGHEST
    rows_all = x_rows.shape[0]
    x_pieces = x_rows.astype(jnp.float32).reshape(rows_all, N_TP, D_DEV)
    g_pieces = g_rows.astype(jnp.float32).reshape(rows_all, N_TP, D_DEV)
    gate = piece_sum(jnp.einsum('rjd,jdf->jrf', x_pieces, weight_g.astype(jnp.float32).reshape(N_TP, D_DEV, HALF), precision=hi))
    up_val = piece_sum(jnp.einsum('rjd,jdf->jrf', x_pieces, weight_u.astype(jnp.float32).reshape(N_TP, D_DEV, HALF), precision=hi))
    d_hidden = piece_sum(jnp.einsum('rjd,fjd->jrf', g_pieces, weight_d.astype(jnp.float32).reshape(HALF, N_TP, D_DEV), precision=hi))
    sig_gate = jax.nn.sigmoid(gate)
    activated = gate * sig_gate
    hidden = (activated * up_val).astype(jnp.bfloat16)
    d_gate = (d_hidden * up_val * sig_gate * (1.0 + gate * (1.0 - sig_gate))).astype(jnp.bfloat16)
    d_up = (d_hidden * activated).astype(jnp.bfloat16)
    grad_wd = jnp.dot(hidden.T, g_rows, preferred_element_type=jnp.float32).astype(jnp.bfloat16)
    grad_wg = jnp.dot(x_rows.T, d_gate, preferred_element_type=jnp.float32).astype(jnp.bfloat16)
    grad_wu = jnp.dot(x_rows.T, d_up, preferred_element_type=jnp.float32).astype(jnp.bfloat16)
    out_half = jnp.dot(hidden, weight_d, preferred_element_type=jnp.float32).astype(jnp.bfloat16)
    back_half = (jnp.dot(d_gate, weight_g.T, preferred_element_type=jnp.float32)
                 + jnp.dot(d_up, weight_u.T, preferred_element_type=jnp.float32)).astype(jnp.bfloat16)
    return grad_wg, grad_wu, grad_wd, out_half, back_half


def reference(tokens, grad_out, routes, route_weight, w_gate, w_up, w_down):
    groups = N_NODE * N_LOCAL
    rows_all = groups * CAP
    hi = lax.Precision.HIGHEST
    x_groups = tokens.reshape(groups, TOK_DEV, D).astype(jnp.float32)
    dy_groups = grad_out.reshape(groups, TOK_DEV, D).astype(jnp.float32)
    w_groups = route_weight.reshape(groups, TOK_DEV * TOPK)
    tables = jax.vmap(lambda r: slot_table(r, EXPERTS, CAP))(routes.reshape(groups, TOK_DEV, TOPK))

    def expert_step(carry, expert):
        y_acc, dx_acc = carry
        select = lax.dynamic_slice_in_dim(tables, expert * CAP, CAP, axis=1)
        token_map = select.reshape(groups, CAP, TOK_DEV, TOPK).sum(-1)
        x_rows = jnp.einsum('gct,gtd->gcd', token_map, x_groups, precision=hi).astype(jnp.bfloat16).reshape(rows_all, D)
        w_sel = jnp.sum(select * w_groups[:, None, :], axis=-1)
        dy_rows = jnp.einsum('gct,gtd->gcd', token_map, dy_groups, precision=hi)
        g_rows = (w_sel[..., None] * dy_rows).astype(jnp.bfloat16).reshape(rows_all, D)
        results = []
        for half in range(2):
            index = (2 * expert + half).astype(jnp.int32)
            weight_g = lax.dynamic_index_in_dim(w_gate, index, 0, keepdims=False)
            weight_u = lax.dynamic_index_in_dim(w_up, index, 0, keepdims=False)
            weight_d = lax.dynamic_index_in_dim(w_down, index, 0, keepdims=False)
            results.append(half_pass(x_rows, g_rows, weight_g, weight_u, weight_d))
        row_out = (results[0][3].astype(jnp.float32) + results[1][3].astype(jnp.float32)).astype(jnp.bfloat16)
        row_back = (results[0][4].astype(jnp.float32) + results[1][4].astype(jnp.float32)).astype(jnp.bfloat16)
        row_out = lax.optimization_barrier(row_out).astype(jnp.float32).reshape(groups, CAP, D)
        row_back = lax.optimization_barrier(row_back).astype(jnp.float32).reshape(groups, CAP, D)
        y_acc = y_acc + jnp.einsum('gct,gcd->gtd', token_map, w_sel[..., None] * row_out, precision=hi)
        dx_acc = dx_acc + jnp.einsum('gct,gcd->gtd', token_map, row_back, precision=hi)
        outs = (jnp.stack([results[0][0], results[1][0]]),
                jnp.stack([results[0][1], results[1][1]]),
                jnp.stack([results[0][2], results[1][2]]))
        return (y_acc, dx_acc), outs

    start = (jnp.zeros((groups, TOK_DEV, D), jnp.float32), jnp.zeros((groups, TOK_DEV, D), jnp.float32))
    (y_acc, dx_acc), (all_gate, all_up, all_down) = lax.scan(expert_step, start, jnp.arange(EXPERTS, dtype=jnp.int32))
    mixed = y_acc.reshape(TOKENS, D).astype(jnp.bfloat16)
    grad_tokens = dx_acc.reshape(TOKENS, D).astype(jnp.bfloat16)
    return (mixed, grad_tokens, all_gate.reshape(2 * EXPERTS, D, HALF),
            all_up.reshape(2 * EXPERTS, D, HALF), all_down.reshape(2 * EXPERTS, HALF, D))
```

```python
import jax
import jax.numpy as jnp
from jax import lax
from jax.experimental import pallas as pl
from jax.experimental.pallas import tpu as pltpu
from jax.sharding import PartitionSpec as P

MESH = pl.DeviceIdType.MESH
F32 = jnp.float32
BF16 = jnp.bfloat16
CAP = 3
CHUNKS = 2

LAST = (((1,), (1,)), ((), ()))
FIRST = (((0,), (0,)), ((), ()))


def mm(a, b, dims=(((1,), (0,)), ((), ()))):
    return lax.dot_general(a, b, dims, preferred_element_type=F32)


def make_kernel(ring, n_local, n_tp, tok_rows, topk, feat, half):
    experts = ring * n_local
    per_chunk = ring // CHUNKS
    rows = per_chunk * CAP
    plane = 2 * n_local
    n_exp = n_local
    all_rows = plane * rows
    part = all_rows // n_tp
    plus = ring // 2 - 1
    minus = ring // 2
    deltas = [(dc, dl) for dl in range(n_local) for dc in range(2) if (dc, dl) != (0, 0)]

    def kernel(
        tok_ref, grd_ref, rt_ref, rw_ref, wg_hbm, wu_hbm, wd_hbm,
        mixed_ref, gtok_ref, gg_ref, gu_ref, gd_ref,
        wg, wu, wd, btok, bgrd, bmeta, sel_s, sel_w, sel, xg, parts, got, acts,
        acc_g, acc_u, acc_d, ob, rob, c_mix, c_back, s_mix, s_back, r_mix, r_back,
        w_sem, ag_send, ag_recv, y_send, y_recv, x_send, x_recv, a_send, a_recv,
        o_send, o_recv, rs_send, rs_recv, own_sem,
    ):
        node = lax.axis_index("node")
        l = lax.axis_index("local")
        j = lax.axis_index("tp")
        z, c = node // 2, node % 2
        slot = c * n_local + l
        up = (lax.rem(z + 1, ring) * 2 + c, l, j)
        down = (lax.rem(z + ring - 1, ring) * 2 + c, l, j)

        def mate(dc, dl):
            cc, ll = lax.rem(c + dc, 2), lax.rem(l + dl, n_local)
            return cc, ll, (z * 2 + cc, ll, j)

        def peer(dj):
            jj = lax.rem(j + dj, n_tp)
            return jj, (node, l, jj)

        loads = [
            pltpu.make_async_copy(src.at[0], dst, w_sem.at[i])
            for i, (src, dst) in enumerate(((wg_hbm, wg), (wu_hbm, wu), (wd_hbm, wd)))
        ]
        for load in loads:
            load.start()

        barrier = pltpu.get_barrier_semaphore()
        partners = [up, down]
        partners += [mate(dc, dl)[2] for dc, dl in deltas]
        partners += [peer(dj)[1] for dj in range(1, n_tp)]
        for who in partners:
            pl.semaphore_signal(barrier, inc=1, device_id=who, device_id_type=MESH)
        pl.semaphore_wait(barrier, len(partners))

        bufs = (btok, bgrd, bmeta)

        def hop(way, s, item, src=None):
            buf = bufs[item]
            if way == 0:
                a, b, who = 2 * s - 1, 2 * s + 1, up
            else:
                a, b, who = 2 * s, 2 * s + 2, down
            return pltpu.make_async_remote_copy(
                src_ref=buf.at[a] if src is None else src,
                dst_ref=buf.at[b],
                send_sem=ag_send.at[way, s, item],
                recv_sem=ag_recv.at[way, s, item],
                device_id=who,
                device_id_type=MESH,
            )

        for item, src in ((0, tok_ref), (1, grd_ref)):
            for way in range(2):
                hop(way, 0, item, src).start()
        btok[0] = tok_ref[...]
        bgrd[0] = grd_ref[...]

        lanes = lax.broadcasted_iota(jnp.int32, (tok_rows, experts), 1)
        named = jnp.zeros((tok_rows, experts), F32)
        weight = jnp.zeros((tok_rows, experts), F32)
        for k in range(topk):
            hit = rt_ref[:, k : k + 1] == lanes
            named = named + hit.astype(F32)
            weight = weight + jnp.where(hit, rw_ref[:, k : k + 1], 0.0)
        before = lax.broadcasted_iota(jnp.int32, (tok_rows, tok_rows), 0) > lax.broadcasted_iota(
            jnp.int32, (tok_rows, tok_rows), 1
        )
        rank = mm(before.astype(F32).astype(BF16), named.astype(BF16))
        t_index = lax.broadcasted_iota(jnp.int32, (tok_rows, experts), 0).astype(F32)
        lines = []
        for cap in range(CAP):
            here = jnp.where(rank == cap, named, 0.0)
            lines.append(jnp.sum(here * (t_index + 1.0), axis=0, keepdims=True) - 1.0)
        for cap in range(CAP):
            here = jnp.where(rank == cap, named, 0.0)
            lines.append(jnp.sum(here * weight, axis=0, keepdims=True))
        lines.append(jnp.zeros((2, experts), F32))
        bmeta[0] = jnp.concatenate(lines, axis=0)
        for way in range(2):
            hop(way, 0, 2, bmeta.at[0]).start()

        def relay(s, _):
            for item in range(3):
                for way in range(2):
                    hop(way, s - 1, item, bufs[item].at[0]).wait_recv()
                    hop(way, s, item).start()
            return 0

        def pick(h):
            base = h * per_chunk
            e_lane = lax.broadcasted_iota(jnp.int32, (per_chunk, experts), 1)
            q = lax.broadcasted_iota(jnp.int32, (per_chunk, 1), 0)
            wide = lax.broadcasted_iota(jnp.int32, (per_chunk, per_chunk * tok_rows), 1)
            for cap in range(CAP):
                idx_all = bmeta[base : base + per_chunk, cap, :]
                w_all = bmeta[base : base + per_chunk, CAP + cap, :]
                for i in range(n_exp):
                    mine = e_lane == z * n_exp + i
                    idx = jnp.sum(jnp.where(mine, idx_all, 0.0), axis=1, keepdims=True)
                    w = jnp.sum(jnp.where(mine, w_all, 0.0), axis=1, keepdims=True)
                    idx = idx.astype(jnp.int32)
                    target = jnp.where(idx >= 0, q * tok_rows + idx, -1)
                    at = i * rows + cap * per_chunk
                    sel_s[h, at : at + per_chunk, :] = (wide == target).astype(F32).astype(BF16)
                    sel_w[h, at : at + per_chunk, :] = jnp.broadcast_to(w, (per_chunk, 128))
            s = sel_s[h]
            x = mm(s, btok[base : base + per_chunk].reshape(per_chunk * tok_rows, feat))
            g = mm(s, bgrd[base : base + per_chunk].reshape(per_chunk * tok_rows, feat))
            g = g * sel_w[h][:, 0:1]
            for i in range(n_exp):
                sel[h, i, 0] = x[i * rows : (i + 1) * rows].astype(BF16)
                sel[h, i, 1] = g[i * rows : (i + 1) * rows].astype(BF16)

        def y_copy(h, d):
            dc, dl = deltas[d]
            cc, ll, who = mate(dc, dl)
            return pltpu.make_async_remote_copy(
                src_ref=sel.at[h, cc * 2 + ll // 2],
                dst_ref=xg.at[h, slot],
                send_sem=y_send.at[h, d],
                recv_sem=y_recv.at[h, d],
                device_id=who,
                device_id_type=MESH,
            )

        def y_arrival(h, d):
            dc, dl = deltas[d]
            cc, ll, who = mate(2 - dc, n_local - dl)
            return pltpu.make_async_remote_copy(
                src_ref=sel.at[h, 0],
                dst_ref=xg.at[h, cc * n_local + ll],
                send_sem=y_send.at[h, d],
                recv_sem=y_recv.at[h, d],
                device_id=who,
                device_id_type=MESH,
            )

        def y_out(h):
            for d in range(len(deltas)):
                y_copy(h, d).start()
            pltpu.make_async_copy(sel.at[h, c * 2 + l // 2], xg.at[h, slot], own_sem.at[h]).start()

        def x_copy(h, dj):
            jj, who = peer(dj)
            return pltpu.make_async_remote_copy(
                src_ref=parts.at[h, jj],
                dst_ref=got.at[h, dj - 1],
                send_sem=x_send.at[h, dj - 1],
                recv_sem=x_recv.at[h, dj - 1],
                device_id=who,
                device_id_type=MESH,
            )

        def first_matmuls(h):
            for d in range(len(deltas)):
                y_arrival(h, d).wait_recv()
            pltpu.make_async_copy(sel.at[h, c * 2 + l // 2], xg.at[h, slot], own_sem.at[h]).wait()
            x = xg[h, :, 0].reshape(all_rows, feat)
            g = xg[h, :, 1].reshape(all_rows, feat)
            parts[h, :, 0] = mm(x, wg[...]).astype(BF16).reshape(n_tp, part, half)
            parts[h, :, 1] = mm(x, wu[...]).astype(BF16).reshape(n_tp, part, half)
            parts[h, :, 2] = mm(g, wd[...], LAST).astype(BF16).reshape(n_tp, part, half)
            for dj in range(1, n_tp):
                x_copy(h, dj).start()

        def a_copy(h, dj, arrival=False):
            jj, who = peer(dj)
            at = lax.rem(j + n_tp - dj, n_tp) if arrival else j
            return pltpu.make_async_remote_copy(
                src_ref=acts.at[h, j],
                dst_ref=acts.at[h, at],
                send_sem=a_send.at[h, dj - 1],
                recv_sem=a_recv.at[h, dj - 1],
                device_id=who,
                device_id_type=MESH,
            )

        def activation(h):
            for dj in range(1, n_tp):
                x_copy(h, dj).wait_recv()
            total = []
            for kind in range(3):
                value = parts[h, j, kind].astype(F32)
                for dj in range(1, n_tp):
                    value = value + got[h, dj - 1, kind].astype(F32)
                total.append(value)
            gate, up_val, d_hidden = total
            sig = jax.nn.sigmoid(gate)
            act = gate * sig
            acts[h, j, 0] = (act * up_val).astype(BF16)
            acts[h, j, 1] = (d_hidden * up_val * sig * (1.0 + gate * (1.0 - sig))).astype(BF16)
            acts[h, j, 2] = (d_hidden * act).astype(BF16)
            for dj in range(1, n_tp):
                a_copy(h, dj).start()

        def o_copy(h, d):
            dc, dl = deltas[d]
            cc, ll, who = mate(dc, dl)
            return pltpu.make_async_remote_copy(
                src_ref=ob.at[h, cc * n_local + ll],
                dst_ref=rob.at[h, slot],
                send_sem=o_send.at[h, d],
                recv_sem=o_recv.at[h, d],
                device_id=who,
                device_id_type=MESH,
            )

        def o_arrival(h, d):
            dc, dl = deltas[d]
            cc, ll, who = mate(2 - dc, n_local - dl)
            return pltpu.make_async_remote_copy(
                src_ref=ob.at[h, 0],
                dst_ref=rob.at[h, cc * n_local + ll],
                send_sem=o_send.at[h, d],
                recv_sem=o_recv.at[h, d],
                device_id=who,
                device_id_type=MESH,
            )

        def own_out(h):
            return pltpu.make_async_copy(ob.at[h, slot], rob.at[h, slot], own_sem.at[CHUNKS + h])

        def last_matmuls(h):
            for dj in range(1, n_tp):
                a_copy(h, dj, True).wait_recv()
            hidden = acts[h, :, 0].reshape(all_rows, half)
            d_gate = acts[h, :, 1].reshape(all_rows, half)
            d_up = acts[h, :, 2].reshape(all_rows, half)
            ob[h, :, 0] = mm(hidden, wd[...]).astype(BF16).reshape(plane, rows, feat)
            back = mm(d_gate, wg[...], LAST) + mm(d_up, wu[...], LAST)
            ob[h, :, 1] = back.astype(BF16).reshape(plane, rows, feat)
            for d in range(len(deltas)):
                o_copy(h, d).start()
            own_out(h).start()

        def weight_grads(h):
            x = xg[h, :, 0].reshape(all_rows, feat)
            g = xg[h, :, 1].reshape(all_rows, feat)
            hidden = acts[h, :, 0].reshape(all_rows, half)
            d_gate = acts[h, :, 1].reshape(all_rows, half)
            d_up = acts[h, :, 2].reshape(all_rows, half)
            for acc, out, a, b in (
                (acc_d, gd_ref, hidden, g),
                (acc_g, gg_ref, x, d_gate),
                (acc_u, gu_ref, x, d_up),
            ):
                value = mm(a, b, FIRST)
                if h > 0:
                    value = acc[...] + value
                if h < CHUNKS - 1:
                    acc[...] = value
                else:
                    out[0] = value.astype(BF16)

        def contributions(h):
            for d in range(len(deltas)):
                o_arrival(h, d).wait_recv()
            own_out(h).wait()
            base = h * per_chunk
            s = sel_s[h]
            outs, backs = [], []
            for i in range(n_exp):
                for kind, keep in ((0, outs), (1, backs)):
                    value = rob[h, 2 * i, kind].astype(F32) + rob[h, 2 * i + 1, kind].astype(F32)
                    keep.append(value.astype(BF16))
            row_out = jnp.concatenate(outs, axis=0).astype(F32) * sel_w[h][:, 0:1]
            high = row_out.astype(BF16)
            low = (row_out - high.astype(F32)).astype(BF16)
            mix = mm(s, high, FIRST) + mm(s, low, FIRST)
            c_mix[base : base + per_chunk] = mix.reshape(per_chunk, tok_rows, feat)
            back = mm(s, jnp.concatenate(backs, axis=0), FIRST)
            c_back[base : base + per_chunk] = back.reshape(per_chunk, tok_rows, feat)

        lax.fori_loop(1, per_chunk // 2 + 1, relay, 0)
        pick(0)
        y_out(0)
        lax.fori_loop(per_chunk // 2 + 1, per_chunk // 2 + 6, relay, 0)
        for load in loads:
            load.wait()
        first_matmuls(0)
        lax.fori_loop(per_chunk // 2 + 6, plus, relay, 0)
        for item in range(3):
            hop(0, plus - 1, item).wait_recv()
            hop(0, plus, item).start()
            hop(1, plus - 1, item).wait_recv()
        for item in range(3):
            hop(0, plus, item).wait_recv()
        pick(1)
        y_out(1)
        activation(0)
        first_matmuls(1)
        last_matmuls(0)
        weight_grads(0)
        activation(1)
        contributions(0)
        last_matmuls(1)
        weight_grads(1)
        contributions(1)

        pieces = ((c_mix, s_mix, r_mix), (c_back, s_back, r_back))

        def fold(way, s, item):
            _, send, receive = pieces[item]
            return pltpu.make_async_remote_copy(
                src_ref=send.at[way, s],
                dst_ref=receive.at[way, s],
                send_sem=rs_send.at[way, s, item],
                recv_sem=rs_recv.at[way, s, item],
                device_id=up if way == 0 else down,
                device_id_type=MESH,
            )

        def place(way, s):
            return 2 * (plus - s) if way == 0 else 2 * (minus - s) - 1

        for way in range(2):
            for item in range(2):
                contrib, send, _ = pieces[item]
                send[way, 0] = contrib[place(way, 0)].astype(BF16)
                fold(way, 0, item).start()

        def add_on(way, s, item):
            contrib, send, receive = pieces[item]
            fold(way, s - 1, item).wait_recv()
            value = contrib[place(way, s)] + receive[way, s - 1].astype(F32)
            send[way, s] = value.astype(BF16)
            fold(way, s, item).start()

        def fold_step(s, _):
            for item in range(2):
                for way in range(2):
                    add_on(way, s, item)
            return 0

        lax.fori_loop(1, plus, fold_step, 0)
        for item in range(2):
            add_on(1, plus, item)
        for item, out in ((0, mixed_ref), (1, gtok_ref)):
            contrib, _, receive = pieces[item]
            fold(0, plus - 1, item).wait_recv()
            fold(1, minus - 1, item).wait_recv()
            value = contrib[0] + receive[0, plus - 1].astype(F32)
            value = value + receive[1, minus - 1].astype(F32)
            out[...] = value.astype(BF16)

        def drain(s, _):
            for item in range(3):
                for way in range(2):
                    hop(way, s, item, bufs[item].at[0]).wait_send()
            for item in range(2):
                for way in range(2):
                    fold(way, s, item).wait_send()
            return 0

        lax.fori_loop(0, plus, drain, 0)
        for item in range(3):
            hop(0, plus, item).wait_send()
        for item in range(2):
            fold(1, plus, item).wait_send()
        for h in range(CHUNKS):
            for d in range(len(deltas)):
                y_copy(h, d).wait_send()
                o_copy(h, d).wait_send()
            for dj in range(1, n_tp):
                x_copy(h, dj).wait_send()
                a_copy(h, dj).wait_send()

    scratch = [
        pltpu.VMEM((feat, half), BF16),
        pltpu.VMEM((feat, half), BF16),
        pltpu.VMEM((half, feat), BF16),
        pltpu.VMEM((ring, tok_rows, feat), BF16),
        pltpu.VMEM((ring, tok_rows, feat), BF16),
        pltpu.VMEM((ring, 8, experts), F32),
        pltpu.VMEM((CHUNKS, n_exp * rows, per_chunk * tok_rows), BF16),
        pltpu.VMEM((CHUNKS, n_exp * rows, 128), F32),
        pltpu.VMEM((CHUNKS, n_exp, 2, rows, feat), BF16),
        pltpu.VMEM((CHUNKS, plane, 2, rows, feat), BF16),
        pltpu.VMEM((CHUNKS, n_tp, 3, part, half), BF16),
        pltpu.VMEM((CHUNKS, n_tp - 1, 3, part, half), BF16),
        pltpu.VMEM((CHUNKS, n_tp, 3, part, half), BF16),
        pltpu.VMEM((feat, half), F32),
        pltpu.VMEM((feat, half), F32),
        pltpu.VMEM((half, feat), F32),
        pltpu.VMEM((CHUNKS, plane, 2, rows, feat), BF16),
        pltpu.VMEM((CHUNKS, plane, 2, rows, feat), BF16),
        pltpu.VMEM((ring, tok_rows, feat), F32),
        pltpu.VMEM((ring, tok_rows, feat), F32),
        pltpu.VMEM((2, minus, tok_rows, feat), BF16),
        pltpu.VMEM((2, minus, tok_rows, feat), BF16),
        pltpu.VMEM((2, minus, tok_rows, feat), BF16),
        pltpu.VMEM((2, minus, tok_rows, feat), BF16),
        pltpu.SemaphoreType.DMA((3,)),
        pltpu.SemaphoreType.DMA((2, minus, 3)),
        pltpu.SemaphoreType.DMA((2, minus, 3)),
        pltpu.SemaphoreType.DMA((CHUNKS, plane - 1)),
        pltpu.SemaphoreType.DMA((CHUNKS, plane - 1)),
        pltpu.SemaphoreType.DMA((CHUNKS, n_tp - 1)),
        pltpu.SemaphoreType.DMA((CHUNKS, n_tp - 1)),
        pltpu.SemaphoreType.DMA((CHUNKS, n_tp - 1)),
        pltpu.SemaphoreType.DMA((CHUNKS, n_tp - 1)),
        pltpu.SemaphoreType.DMA((CHUNKS, plane - 1)),
        pltpu.SemaphoreType.DMA((CHUNKS, plane - 1)),
        pltpu.SemaphoreType.DMA((2, minus, 2)),
        pltpu.SemaphoreType.DMA((2, minus, 2)),
        pltpu.SemaphoreType.DMA((2 * CHUNKS,)),
    ]
    return kernel, scratch


def solution(mesh):
    ring, n_local, n_tp = mesh.shape["node"] // 2, mesh.shape["local"], mesh.shape["tp"]

    def shards(tokens, grad_out, routes, route_weight, w_gate, w_up, w_down):
        tok_rows, feat = tokens.shape
        half = w_gate.shape[2]
        kernel, scratch = make_kernel(ring, n_local, n_tp, tok_rows, routes.shape[1], feat, half)
        vmem = pl.BlockSpec(memory_space=pltpu.VMEM)
        return pl.pallas_call(
            kernel,
            out_shape=(
                jax.ShapeDtypeStruct((tok_rows, feat), BF16),
                jax.ShapeDtypeStruct((tok_rows, feat), BF16),
                jax.ShapeDtypeStruct((1, feat, half), BF16),
                jax.ShapeDtypeStruct((1, feat, half), BF16),
                jax.ShapeDtypeStruct((1, half, feat), BF16),
            ),
            in_specs=[vmem] * 4 + [pl.BlockSpec(memory_space=pl.ANY)] * 3,
            out_specs=(vmem,) * 5,
            scratch_shapes=scratch,
            compiler_params=pltpu.CompilerParams(collective_id=0, has_side_effects=True),
            name="routed_experts",
        )(tokens, grad_out, routes, route_weight, w_gate, w_up, w_down)

    return jax.shard_map(
        shards,
        mesh=mesh,
        in_specs=(
            P(("node", "local"), "tp"),
            P(("node", "local"), "tp"),
            P(("node", "local"), None),
            P(("node", "local"), None),
            P(("node", "local"), "tp", None),
            P(("node", "local"), "tp", None),
            P(("node", "local"), None, "tp"),
        ),
        out_specs=(
            P(("node", "local"), "tp"),
            P(("node", "local"), "tp"),
            P(("node", "local"), "tp", None),
            P(("node", "local"), "tp", None),
            P(("node", "local"), None, "tp"),
        ),
        check_vma=False,
    )
```

```python
import jax
import jax.numpy as jnp
from jax import lax
from jax.experimental import pallas as pl
from jax.experimental.pallas import tpu as pltpu
from jax.sharding import PartitionSpec as P

MESH = pl.DeviceIdType.MESH
F32 = jnp.float32
BF16 = jnp.bfloat16
CAP = 3
CHUNKS = 2

LAST = (((1,), (1,)), ((), ()))
FIRST = (((0,), (0,)), ((), ()))


def mm(a, b, dims=(((1,), (0,)), ((), ()))):
    return lax.dot_general(a, b, dims, preferred_element_type=F32)


def make_kernel(ring, n_local, n_tp, tok_rows, topk, feat, half):
    experts = ring * n_local
    per_chunk = ring // CHUNKS
    rows = per_chunk * CAP
    plane = 2 * n_local
    n_exp = n_local
    all_rows = plane * rows
    part = all_rows // n_tp
    chain = ring // 4
    half_chain = chain // 2

    def even(e):
        return e if e < chain else e + chain

    def odd(way, a):
        near = chain + way * half_chain + a
        return near if a < half_chain else near + chain + half_chain

    deltas = [(dc, dl) for dl in range(n_local) for dc in range(2) if (dc, dl) != (0, 0)]

    def kernel(
        tok_ref, grd_ref, rt_ref, rw_ref, wg_hbm, wu_hbm, wd_hbm,
        mixed_ref, gtok_ref, gg_ref, gu_ref, gd_ref,
        wg, wu, wd, btok, bgrd, bmeta, sel_s, sel_w, sel, xg, parts, got, acts,
        acc_g, acc_u, acc_d, ob, rob, c_mix, c_back,
        s_mix, s_back, r_mix, r_back, t_mix, t_back, n_mix, n_back, o_mix, o_back, o_g, o_u, o_d,
        w_sem, ag_send, ag_recv, y_send, y_recv, x_send, x_recv, a_send, a_recv,
        o_send, o_recv, rs_send, rs_recv, own_sem, sh_send, sh_recv, ln_send, ln_recv,
    ):
        node = lax.axis_index("node")
        l = lax.axis_index("local")
        j = lax.axis_index("tp")
        z, c = node // 2, node % 2
        slot = c * n_local + l

        def along(step):
            return (lax.rem(z + ring + step, ring) * 2 + c, l, j)

        two = (along(2), along(-2))
        one = (along(1), along(-1))

        def mate(dc, dl):
            cc, ll = lax.rem(c + dc, 2), lax.rem(l + dl, n_local)
            return cc, ll, (z * 2 + cc, ll, j)

        def peer(dj):
            jj = lax.rem(j + dj, n_tp)
            return jj, (node, l, jj)

        loads = [
            pltpu.make_async_copy(src.at[0], dst, w_sem.at[i])
            for i, (src, dst) in enumerate(((wg_hbm, wg), (wu_hbm, wu), (wd_hbm, wd)))
        ]
        for load in loads:
            load.start()

        barrier = pltpu.get_barrier_semaphore()
        partners = [*two, *one]
        partners += [mate(dc, dl)[2] for dc, dl in deltas]
        partners += [peer(dj)[1] for dj in range(1, n_tp)]
        for who in partners:
            pl.semaphore_signal(barrier, inc=1, device_id=who, device_id_type=MESH)
        pl.semaphore_wait(barrier, len(partners))

        bufs = (btok, bgrd, bmeta)

        def carried(way, s):
            return even(0) if s == 0 else even(2 * s - 1 + way)

        def hop(way, s, item, src=None):
            buf = bufs[item]
            return pltpu.make_async_remote_copy(
                src_ref=buf.at[carried(way, s)] if src is None else src,
                dst_ref=buf.at[even(2 * s + 1 + way)],
                send_sem=ag_send.at[way, s, item],
                recv_sem=ag_recv.at[way, s, item],
                device_id=two[way],
                device_id_type=MESH,
            )

        def share(way, s, item, src=None):
            buf = bufs[item]
            return pltpu.make_async_remote_copy(
                src_ref=buf.at[carried(way, s)] if src is None else src,
                dst_ref=buf.at[odd(way, s)],
                send_sem=sh_send.at[way, s, item],
                recv_sem=sh_recv.at[way, s, item],
                device_id=one[way],
                device_id_type=MESH,
            )

        for item, src in ((0, tok_ref), (1, grd_ref)):
            for way in range(2):
                hop(way, 0, item, src).start()
        for item, src in ((0, tok_ref), (1, grd_ref)):
            for way in range(2):
                share(way, 0, item, src).start()
        btok[0] = tok_ref[...]
        bgrd[0] = grd_ref[...]

        lanes = lax.broadcasted_iota(jnp.int32, (tok_rows, experts), 1)
        named = jnp.zeros((tok_rows, experts), F32)
        weight = jnp.zeros((tok_rows, experts), F32)
        rt = jnp.transpose(rt_ref[...].astype(F32)).astype(jnp.int32)
        rw = jnp.transpose(rw_ref[...])
        for k in range(topk):
            hit = rt[:, k : k + 1] == lanes
            named = named + hit.astype(F32)
            weight = weight + jnp.where(hit, rw[:, k : k + 1], 0.0)
        before = lax.broadcasted_iota(jnp.int32, (tok_rows, tok_rows), 0) > lax.broadcasted_iota(
            jnp.int32, (tok_rows, tok_rows), 1
        )
        rank = mm(before.astype(F32).astype(BF16), named.astype(BF16))
        t_index = lax.broadcasted_iota(jnp.int32, (tok_rows, experts), 0).astype(F32)
        lines = []
        for cap in range(CAP):
            here = jnp.where(rank == cap, named, 0.0)
            lines.append(jnp.sum(here * (t_index + 1.0), axis=0, keepdims=True) - 1.0)
        for cap in range(CAP):
            here = jnp.where(rank == cap, named, 0.0)
            lines.append(jnp.sum(here * weight, axis=0, keepdims=True))
        lines.append(jnp.zeros((2, experts), F32))
        bmeta[0] = jnp.concatenate(lines, axis=0)
        for way in range(2):
            hop(way, 0, 2).start()
            share(way, 0, 2).start()

        def relay(s):
            ways = [way for way in range(2) if way == 0 or s < chain]
            for item in range(3):
                for way in ways:
                    hop(way, s - 1, item).wait_recv()
                    if s < chain - way:
                        hop(way, s, item).start()
            if s < chain:
                for item in range(3):
                    for way in range(2):
                        share(way, s, item).start()

        def shared(first, last):
            for s in range(first, last):
                for item in range(3):
                    for way in range(2):
                        share(way, s, item).wait_recv()

        def pick(h):
            base = h * per_chunk
            e_lane = lax.broadcasted_iota(jnp.int32, (per_chunk, experts), 1)
            q = lax.broadcasted_iota(jnp.int32, (per_chunk, 1), 0)
            wide = lax.broadcasted_iota(jnp.int32, (per_chunk, per_chunk * tok_rows), 1)
            for cap in range(CAP):
                idx_all = bmeta[base : base + per_chunk, cap, :]
                w_all = bmeta[base : base + per_chunk, CAP + cap, :]
                for i in range(n_exp):
                    mine = e_lane == z * n_exp + i
                    idx = jnp.sum(jnp.where(mine, idx_all, 0.0), axis=1, keepdims=True)
                    w = jnp.sum(jnp.where(mine, w_all, 0.0), axis=1, keepdims=True)
                    idx = idx.astype(jnp.int32)
                    target = jnp.where(idx >= 0, q * tok_rows + idx, -1)
                    at = i * rows + cap * per_chunk
                    sel_s[h, at : at + per_chunk, :] = (wide == target).astype(F32).astype(BF16)
                    sel_w[h, at : at + per_chunk, :] = jnp.broadcast_to(w, (per_chunk, 128))
            s = sel_s[h]
            x = mm(s, btok[base : base + per_chunk].reshape(per_chunk * tok_rows, feat))
            g = mm(s, bgrd[base : base + per_chunk].reshape(per_chunk * tok_rows, feat))
            g = g * sel_w[h][:, 0:1]
            for i in range(n_exp):
                sel[h, i, 0] = x[i * rows : (i + 1) * rows].astype(BF16)
                sel[h, i, 1] = g[i * rows : (i + 1) * rows].astype(BF16)

        def y_copy(h, d):
            dc, dl = deltas[d]
            cc, ll, who = mate(dc, dl)
            return pltpu.make_async_remote_copy(
                src_ref=sel.at[h, cc * 2 + ll // 2],
                dst_ref=xg.at[h, slot],
                send_sem=y_send.at[h, d],
                recv_sem=y_recv.at[h, d],
                device_id=who,
                device_id_type=MESH,
            )

        def y_arrival(h, d):
            dc, dl = deltas[d]
            cc, ll, who = mate(2 - dc, n_local - dl)
            return pltpu.make_async_remote_copy(
                src_ref=sel.at[h, 0],
                dst_ref=xg.at[h, cc * n_local + ll],
                send_sem=y_send.at[h, d],
                recv_sem=y_recv.at[h, d],
                device_id=who,
                device_id_type=MESH,
            )

        def y_out(h):
            for d in range(len(deltas)):
                y_copy(h, d).start()
            pltpu.make_async_copy(sel.at[h, c * 2 + l // 2], xg.at[h, slot], own_sem.at[h]).start()

        def x_copy(h, dj):
            jj, who = peer(dj)
            return pltpu.make_async_remote_copy(
                src_ref=parts.at[h, jj],
                dst_ref=got.at[h, dj - 1],
                send_sem=x_send.at[h, dj - 1],
                recv_sem=x_recv.at[h, dj - 1],
                device_id=who,
                device_id_type=MESH,
            )

        def first_matmuls(h):
            for d in range(len(deltas)):
                y_arrival(h, d).wait_recv()
            pltpu.make_async_copy(sel.at[h, c * 2 + l // 2], xg.at[h, slot], own_sem.at[h]).wait()
            x = xg[h, :, 0].reshape(all_rows, feat)
            g = xg[h, :, 1].reshape(all_rows, feat)
            parts[h, :, 0] = mm(x, wg[...]).astype(BF16).reshape(n_tp, part, half)
            parts[h, :, 1] = mm(x, wu[...]).astype(BF16).reshape(n_tp, part, half)
            parts[h, :, 2] = mm(g, wd[...], LAST).astype(BF16).reshape(n_tp, part, half)
            for dj in range(1, n_tp):
                x_copy(h, dj).start()

        def a_copy(h, dj, arrival=False):
            jj, who = peer(dj)
            at = lax.rem(j + n_tp - dj, n_tp) if arrival else j
            return pltpu.make_async_remote_copy(
                src_ref=acts.at[h, j],
                dst_ref=acts.at[h, at],
                send_sem=a_send.at[h, dj - 1],
                recv_sem=a_recv.at[h, dj - 1],
                device_id=who,
                device_id_type=MESH,
            )

        def activation(h):
            for dj in range(1, n_tp):
                x_copy(h, dj).wait_recv()
            total = []
            for kind in range(3):
                value = parts[h, j, kind].astype(F32)
                for dj in range(1, n_tp):
                    value = value + got[h, dj - 1, kind].astype(F32)
                total.append(value)
            gate, up_val, d_hidden = total
            sig = jax.nn.sigmoid(gate)
            act = gate * sig
            acts[h, j, 0] = (act * up_val).astype(BF16)
            acts[h, j, 1] = (d_hidden * up_val * sig * (1.0 + gate * (1.0 - sig))).astype(BF16)
            acts[h, j, 2] = (d_hidden * act).astype(BF16)
            for dj in range(1, n_tp):
                a_copy(h, dj).start()

        def o_copy(h, d):
            dc, dl = deltas[d]
            cc, ll, who = mate(dc, dl)
            return pltpu.make_async_remote_copy(
                src_ref=ob.at[h, cc * n_local + ll],
                dst_ref=rob.at[h, slot],
                send_sem=o_send.at[h, d],
                recv_sem=o_recv.at[h, d],
                device_id=who,
                device_id_type=MESH,
            )

        def o_arrival(h, d):
            dc, dl = deltas[d]
            cc, ll, who = mate(2 - dc, n_local - dl)
            return pltpu.make_async_remote_copy(
                src_ref=ob.at[h, 0],
                dst_ref=rob.at[h, cc * n_local + ll],
                send_sem=o_send.at[h, d],
                recv_sem=o_recv.at[h, d],
                device_id=who,
                device_id_type=MESH,
            )

        def own_out(h):
            return pltpu.make_async_copy(ob.at[h, slot], rob.at[h, slot], own_sem.at[CHUNKS + h])

        def last_matmuls(h):
            for dj in range(1, n_tp):
                a_copy(h, dj, True).wait_recv()
            hidden = acts[h, :, 0].reshape(all_rows, half)
            d_gate = acts[h, :, 1].reshape(all_rows, half)
            d_up = acts[h, :, 2].reshape(all_rows, half)
            ob[h, :, 0] = mm(hidden, wd[...]).astype(BF16).reshape(plane, rows, feat)
            back = mm(d_gate, wg[...], LAST) + mm(d_up, wu[...], LAST)
            ob[h, :, 1] = back.astype(BF16).reshape(plane, rows, feat)
            for d in range(len(deltas)):
                o_copy(h, d).start()
            own_out(h).start()

        def weight_grads(h):
            x = xg[h, :, 0].reshape(all_rows, feat)
            g = xg[h, :, 1].reshape(all_rows, feat)
            hidden = acts[h, :, 0].reshape(all_rows, half)
            d_gate = acts[h, :, 1].reshape(all_rows, half)
            d_up = acts[h, :, 2].reshape(all_rows, half)
            for acc, out, a, b in (
                (acc_d, o_d, hidden, g),
                (acc_g, o_g, x, d_gate),
                (acc_u, o_u, x, d_up),
            ):
                value = mm(a, b, FIRST)
                if h > 0:
                    value = acc[...] + value
                if h < CHUNKS - 1:
                    acc[...] = value
                else:
                    out[...] = value.astype(BF16)

        def contributions(h):
            for d in range(len(deltas)):
                o_arrival(h, d).wait_recv()
            own_out(h).wait()
            base = h * per_chunk
            s = sel_s[h]
            outs, backs = [], []
            for i in range(n_exp):
                for kind, keep in ((0, outs), (1, backs)):
                    value = rob[h, 2 * i, kind].astype(F32) + rob[h, 2 * i + 1, kind].astype(F32)
                    keep.append(value.astype(BF16))
            row_out = jnp.concatenate(outs, axis=0).astype(F32) * sel_w[h][:, 0:1]
            high = row_out.astype(BF16)
            low = (row_out - high.astype(F32)).astype(BF16)
            mix = mm(s, high, FIRST) + mm(s, low, FIRST)
            c_mix[base : base + per_chunk] = mix.reshape(per_chunk, tok_rows, feat)
            back = mm(s, jnp.concatenate(backs, axis=0), FIRST)
            c_back[base : base + per_chunk] = back.reshape(per_chunk, tok_rows, feat)

        for s in range(1, half_chain + 1):
            relay(s)
        shared(0, half_chain)
        pick(0)
        y_out(0)
        for s in range(half_chain + 1, chain - 1):
            relay(s)
        for load in loads:
            load.wait()
        first_matmuls(0)
        for s in range(chain - 1, chain + 1):
            relay(s)
        shared(half_chain, chain)
        pick(1)
        y_out(1)
        activation(0)
        first_matmuls(1)
        last_matmuls(0)
        weight_grads(0)
        activation(1)
        contributions(0)
        last_matmuls(1)
        weight_grads(1)
        stores = [
            pltpu.make_async_copy(src, dst.at[0], w_sem.at[3 + i])
            for i, (src, dst) in enumerate(((o_g, gg_ref), (o_u, gu_ref), (o_d, gd_ref)))
        ]
        for store in stores:
            store.start()
        contributions(1)

        pieces = (
            (c_mix, s_mix, r_mix, t_mix, n_mix),
            (c_back, s_back, r_back, t_back, n_back),
        )

        def lend(way, a, item):
            _, _, _, send, receive = pieces[item]
            return pltpu.make_async_remote_copy(
                src_ref=send.at[way, a],
                dst_ref=receive.at[way, a],
                send_sem=ln_send.at[way, a, item],
                recv_sem=ln_recv.at[way, a, item],
                device_id=one[way],
                device_id_type=MESH,
            )

        def fold(way, s, item):
            _, send, receive, _, _ = pieces[item]
            return pltpu.make_async_remote_copy(
                src_ref=send.at[way, s],
                dst_ref=receive.at[way, s],
                send_sem=rs_send.at[way, s, item],
                recv_sem=rs_recv.at[way, s, item],
                device_id=two[way],
                device_id_type=MESH,
            )

        def lend_out(way, a, item):
            contrib, _, _, send, _ = pieces[item]
            send[way, a] = contrib[odd(1 - way, a)].astype(BF16)
            lend(way, a, item).start()

        def add_on(way, away, item):
            contrib, send, receive, _, lent = pieces[item]
            s = chain - away
            value = contrib[even(2 * away - way)]
            if away < chain:
                lend(way, away, item).wait_recv()
                value = value + lent[way, away].astype(F32)
            if away < chain - 1 + way:
                fold(way, s - 1, item).wait_recv()
                value = value + receive[way, s - 1].astype(F32)
            send[way, s] = value.astype(BF16)
            fold(way, s, item).start()

        for item in range(2):
            add_on(1, chain, item)
        for a in range(chain - 1, -1, -1):
            for item in range(2):
                for way in range(2):
                    lend_out(way, a, item)
            if a < chain - 1:
                for item in range(2):
                    for way in range(2):
                        add_on(way, a + 1, item)
        for item, out in ((0, o_mix), (1, o_back)):
            contrib, _, receive, _, lent = pieces[item]
            value = contrib[0]
            for way in range(2):
                lend(way, 0, item).wait_recv()
                value = value + lent[way, 0].astype(F32)
                fold(way, chain - 1, item).wait_recv()
                value = value + receive[way, chain - 1].astype(F32)
            out[...] = value.astype(BF16)
        stores += [
            pltpu.make_async_copy(o_mix, mixed_ref, w_sem.at[6]),
            pltpu.make_async_copy(o_back, gtok_ref, w_sem.at[7]),
        ]
        for store in stores[3:]:
            store.start()

        for s in range(chain):
            for item in range(3):
                for way in range(2):
                    share(way, s, item).wait_send()
                    if s < chain - way:
                        hop(way, s, item).wait_send()
            for item in range(2):
                for way in range(2):
                    lend(way, s, item).wait_send()
                    if s > 0 or way == 1:
                        fold(way, s, item).wait_send()
        for h in range(CHUNKS):
            for d in range(len(deltas)):
                y_copy(h, d).wait_send()
                o_copy(h, d).wait_send()
            for dj in range(1, n_tp):
                x_copy(h, dj).wait_send()
                a_copy(h, dj).wait_send()
        for store in stores:
            store.wait()

    scratch = [
        pltpu.VMEM((feat, half), BF16),
        pltpu.VMEM((feat, half), BF16),
        pltpu.VMEM((half, feat), BF16),
        pltpu.VMEM((ring, tok_rows, feat), BF16),
        pltpu.VMEM((ring, tok_rows, feat), BF16),
        pltpu.VMEM((ring, 8, experts), F32),
        pltpu.VMEM((CHUNKS, n_exp * rows, per_chunk * tok_rows), BF16),
        pltpu.VMEM((CHUNKS, n_exp * rows, 128), F32),
        pltpu.VMEM((CHUNKS, n_exp, 2, rows, feat), BF16),
        pltpu.VMEM((CHUNKS, plane, 2, rows, feat), BF16),
        pltpu.VMEM((CHUNKS, n_tp, 3, part, half), BF16),
        pltpu.VMEM((CHUNKS, n_tp - 1, 3, part, half), BF16),
        pltpu.VMEM((CHUNKS, n_tp, 3, part, half), BF16),
        pltpu.VMEM((feat, half), F32),
        pltpu.VMEM((feat, half), F32),
        pltpu.VMEM((half, feat), F32),
        pltpu.VMEM((CHUNKS, plane, 2, rows, feat), BF16),
        pltpu.VMEM((CHUNKS, plane, 2, rows, feat), BF16),
        pltpu.VMEM((ring, tok_rows, feat), F32),
        pltpu.VMEM((ring, tok_rows, feat), F32),
        *[pltpu.VMEM((2, chain, tok_rows, feat), BF16)] * 8,
        pltpu.VMEM((tok_rows, feat), BF16),
        pltpu.VMEM((tok_rows, feat), BF16),
        pltpu.VMEM((feat, half), BF16),
        pltpu.VMEM((feat, half), BF16),
        pltpu.VMEM((half, feat), BF16),
        pltpu.SemaphoreType.DMA((8,)),
        pltpu.SemaphoreType.DMA((2, chain, 3)),
        pltpu.SemaphoreType.DMA((2, chain, 3)),
        pltpu.SemaphoreType.DMA((CHUNKS, plane - 1)),
        pltpu.SemaphoreType.DMA((CHUNKS, plane - 1)),
        pltpu.SemaphoreType.DMA((CHUNKS, n_tp - 1)),
        pltpu.SemaphoreType.DMA((CHUNKS, n_tp - 1)),
        pltpu.SemaphoreType.DMA((CHUNKS, n_tp - 1)),
        pltpu.SemaphoreType.DMA((CHUNKS, n_tp - 1)),
        pltpu.SemaphoreType.DMA((CHUNKS, plane - 1)),
        pltpu.SemaphoreType.DMA((CHUNKS, plane - 1)),
        pltpu.SemaphoreType.DMA((2, chain, 2)),
        pltpu.SemaphoreType.DMA((2, chain, 2)),
        pltpu.SemaphoreType.DMA((2 * CHUNKS,)),
        pltpu.SemaphoreType.DMA((2, chain, 3)),
        pltpu.SemaphoreType.DMA((2, chain, 3)),
        pltpu.SemaphoreType.DMA((2, chain, 2)),
        pltpu.SemaphoreType.DMA((2, chain, 2)),
    ]
    return kernel, scratch


def deliver(arrays):
    count = len(arrays)

    def kernel(*refs):
        sources, targets, held = refs[:count], refs[count : 2 * count], refs[2 * count : 3 * count]
        in_sem, out_sem = refs[3 * count :]
        loads = [pltpu.make_async_copy(sources[i], held[i], in_sem.at[i]) for i in range(count)]
        stores = [pltpu.make_async_copy(held[i], targets[i], out_sem.at[i]) for i in range(count)]
        for load in loads:
            load.start()
        for load, store in zip(loads, stores):
            load.wait()
            store.start()
        for store in stores:
            store.wait()

    anywhere = pl.BlockSpec(memory_space=pl.ANY)
    return pl.pallas_call(
        kernel,
        out_shape=tuple(jax.ShapeDtypeStruct(a.shape, a.dtype) for a in arrays),
        in_specs=[anywhere] * count,
        out_specs=(anywhere,) * count,
        scratch_shapes=[pltpu.VMEM(a.shape, a.dtype) for a in arrays]
        + [pltpu.SemaphoreType.DMA((count,))] * 2,
        name="deliver",
    )(*arrays)


def solution(mesh):
    ring, n_local, n_tp = mesh.shape["node"] // 2, mesh.shape["local"], mesh.shape["tp"]

    def shards(tokens, grad_out, routes, route_weight, w_gate, w_up, w_down):
        tok_rows, feat = tokens.shape
        half = w_gate.shape[2]
        kernel, scratch = make_kernel(ring, n_local, n_tp, tok_rows, routes.shape[1], feat, half)
        vmem = pl.BlockSpec(memory_space=pltpu.VMEM)
        outs = pl.pallas_call(
            kernel,
            out_shape=(
                jax.ShapeDtypeStruct((tok_rows, feat), BF16),
                jax.ShapeDtypeStruct((tok_rows, feat), BF16),
                jax.ShapeDtypeStruct((1, feat, half), BF16),
                jax.ShapeDtypeStruct((1, feat, half), BF16),
                jax.ShapeDtypeStruct((1, half, feat), BF16),
            ),
            in_specs=[vmem] * 4 + [pl.BlockSpec(memory_space=pl.ANY)] * 3,
            out_specs=(pl.BlockSpec(memory_space=pl.ANY),) * 5,
            scratch_shapes=scratch,
            compiler_params=pltpu.CompilerParams(collective_id=0, has_side_effects=True),
            name="routed_experts",
        )(tokens, grad_out, routes.T, route_weight.T, w_gate, w_up, w_down)
        return deliver(outs)

    return jax.shard_map(
        shards,
        mesh=mesh,
        in_specs=(
            P(("node", "local"), "tp"),
            P(("node", "local"), "tp"),
            P(("node", "local"), None),
            P(("node", "local"), None),
            P(("node", "local"), "tp", None),
            P(("node", "local"), "tp", None),
            P(("node", "local"), None, "tp"),
        ),
        out_specs=(
            P(("node", "local"), "tp"),
            P(("node", "local"), "tp"),
            P(("node", "local"), "tp", None),
            P(("node", "local"), "tp", None),
            P(("node", "local"), None, "tp"),
        ),
        check_vma=False,
    )
```

```python
import jax
import jax.numpy as jnp
from jax import lax
from jax.experimental import pallas as pl
from jax.experimental.pallas import tpu as pltpu
from jax.sharding import PartitionSpec as P

MESH = pl.DeviceIdType.MESH
F32 = jnp.float32
BF16 = jnp.bfloat16
CAP = 3
CHUNKS = 4

SHARED = 16
PARTS = 2

LAST = (((1,), (1,)), ((), ()))
FIRST = (((0,), (0,)), ((), ()))


def mm(a, b, dims=(((1,), (0,)), ((), ()))):
    return lax.dot_general(a, b, dims, preferred_element_type=F32)


def make_kernel(ring, n_local, n_tp, tok_rows, topk, feat, half):
    experts = ring * n_local
    per_chunk = ring // CHUNKS
    rows = per_chunk * CAP
    plane = 2 * n_local
    n_exp = n_local
    all_rows = plane * rows
    strip = all_rows // n_tp
    chain = ring // 4

    quarter = chain // 4

    def even(e):
        return e // (2 * quarter) * per_chunk + e % (2 * quarter)

    def odd(way, a):
        return a // quarter * per_chunk + 2 * quarter + way * quarter + a % quarter

    piece = tok_rows // PARTS
    legs = [(item, part) for item in range(2) for part in range(PARTS)] + [(2, 0)]
    deltas = [(dc, dl) for dl in range(n_local) for dc in range(2) if (dc, dl) != (0, 0)]

    def kernel(
        tok_ref, grd_ref, rt_ref, rw_ref, wg_hbm, wu_hbm, wd_hbm,
        mixed_ref, gtok_ref, gg_ref, gu_ref, gd_ref,
        wg, wu, wd, btok, bgrd, bmeta, sel_s, sel_w, sel, xg, parts, got, acts,
        acc_g, acc_u, acc_d, ob, rob, c_mix, c_back,
        s_mix, s_back, r_mix, r_back, t_mix, t_back, n_mix, n_back, o_mix, o_back, o_g, o_u, o_d,
        w_sem, ag_send, ag_recv, y_send, y_recv, x_send, x_recv, a_send, a_recv,
        o_send, o_recv, rs_send, rs_recv, own_sem, s_odd, lent_rows, odd_rows, sh_send, sh_recv, ln_send, ln_recv,
    ):
        node = lax.axis_index("node")
        l = lax.axis_index("local")
        j = lax.axis_index("tp")
        z, c = node // 2, node % 2
        slot = c * n_local + l

        def along(step):
            return (lax.rem(z + ring + step, ring) * 2 + c, l, j)

        two = (along(2), along(-2))
        one = (along(1), along(-1))

        def mate(dc, dl):
            cc, ll = lax.rem(c + dc, 2), lax.rem(l + dl, n_local)
            return cc, ll, (z * 2 + cc, ll, j)

        def peer(dj):
            jj = lax.rem(j + dj, n_tp)
            return jj, (node, l, jj)

        loads = [
            pltpu.make_async_copy(src.at[0], dst, w_sem.at[i])
            for i, (src, dst) in enumerate(((wg_hbm, wg), (wu_hbm, wu), (wd_hbm, wd)))
        ]
        for load in loads:
            load.start()

        barrier = pltpu.get_barrier_semaphore()
        partners = [*two, *one]
        partners += [mate(dc, dl)[2] for dc, dl in deltas]
        partners += [peer(dj)[1] for dj in range(1, n_tp)]
        for who in partners:
            pl.semaphore_signal(barrier, inc=1, device_id=who, device_id_type=MESH)

        bufs = (btok, bgrd, bmeta)

        def carried(way, s):
            return 0 if s == 0 else 2 * s - 1 + way

        def block(item, e):
            return bmeta.at[even(e)] if item == 2 else bufs[item].at[e]

        def cut(ref, part):
            return ref.at[pl.ds(part * piece, piece)]

        def hop(way, s, leg, first=None):
            item, part = legs[leg]
            src = block(item, carried(way, s)) if first is None else first
            dst = block(item, 2 * s + 1 + way)
            if item < 2:
                src, dst = cut(src, part), cut(dst, part)
            return pltpu.make_async_remote_copy(
                src_ref=src,
                dst_ref=dst,
                send_sem=ag_send.at[item],
                recv_sem=ag_recv.at[way, s, leg],
                device_id=two[way],
                device_id_type=MESH,
            )

        def share(way, s, item):
            if item == 2:
                src, dst = block(2, carried(way, s)), bmeta.at[odd(way, s)]
            else:
                src = lent_rows.at[item, way, s]
                dst = odd_rows.at[item, s // quarter, way * quarter + s % quarter]
            return pltpu.make_async_remote_copy(
                src_ref=src,
                dst_ref=dst,
                send_sem=sh_send.at[item],
                recv_sem=sh_recv.at[way, s, item],
                device_id=one[way],
                device_id_type=MESH,
            )

        def share_out(s):
            for way in range(2):
                share(way, s, 2).start()
            for way in range(2):
                e = carried(way, s)
                theirs = lax.rem(z + ring + (1, -1)[way], ring) * n_exp
                meta = bmeta[even(e)]
                r = lax.broadcasted_iota(jnp.int32, (SHARED, experts), 0)
                lane = lax.broadcasted_iota(jnp.int32, (SHARED, experts), 1)
                value = jnp.full((SHARED, experts), -1.0, F32)
                target = jnp.full((SHARED, experts), -1, jnp.int32)
                for cap in range(CAP):
                    inside = (r >= cap * n_exp) & (r < (cap + 1) * n_exp)
                    value = jnp.where(inside, meta[cap : cap + 1, :], value)
                    target = jnp.where(inside, theirs + r - cap * n_exp, target)
                idx = jnp.sum(jnp.where(lane == target, value + 1.0, 0.0), axis=1, keepdims=True) - 1.0
                t_lane = lax.broadcasted_iota(jnp.int32, (SHARED, tok_rows), 1)
                choose = (t_lane == idx.astype(jnp.int32)).astype(F32).astype(BF16)
                for item in range(2):
                    lent_rows[item, way, s] = mm(choose, bufs[item][e]).astype(BF16)
                    share(way, s, item).start()

        btok[0] = tok_ref[...]
        bgrd[0] = grd_ref[...]

        lanes = lax.broadcasted_iota(jnp.int32, (tok_rows, experts), 1)
        named = jnp.zeros((tok_rows, experts), F32)
        weight = jnp.zeros((tok_rows, experts), F32)
        rt = jnp.transpose(rt_ref[...].astype(F32)).astype(jnp.int32)
        rw = jnp.transpose(rw_ref[...])
        for k in range(topk):
            hit = rt[:, k : k + 1] == lanes
            named = named + hit.astype(F32)
            weight = weight + jnp.where(hit, rw[:, k : k + 1], 0.0)
        before = lax.broadcasted_iota(jnp.int32, (tok_rows, tok_rows), 0) > lax.broadcasted_iota(
            jnp.int32, (tok_rows, tok_rows), 1
        )
        rank = mm(before.astype(F32).astype(BF16), named.astype(BF16))
        t_index = lax.broadcasted_iota(jnp.int32, (tok_rows, experts), 0).astype(F32)
        lines = []
        for cap in range(CAP):
            here = jnp.where(rank == cap, named, 0.0)
            lines.append(jnp.sum(here * (t_index + 1.0), axis=0, keepdims=True) - 1.0)
        for cap in range(CAP):
            here = jnp.where(rank == cap, named, 0.0)
            lines.append(jnp.sum(here * weight, axis=0, keepdims=True))
        lines.append(jnp.zeros((2, experts), F32))
        bmeta[0] = jnp.concatenate(lines, axis=0)
        for cap in range(CAP):
            for i in range(n_exp):
                q = lax.broadcasted_iota(jnp.int32, (per_chunk, 1), 0) - 2 * quarter
                wide = lax.broadcasted_iota(jnp.int32, (per_chunk, 2 * quarter * SHARED), 1)
                target = jnp.where(q >= 0, q * SHARED + cap * n_exp + i, -1)
                at = i * rows + cap * per_chunk
                s_odd[at : at + per_chunk, :] = (wide == target).astype(F32).astype(BF16)
        pl.semaphore_wait(barrier, len(partners))
        for leg, (item, _) in enumerate(legs[:-1]):
            for way in range(2):
                hop(way, 0, leg, (tok_ref, grd_ref)[item]).start()
        for way in range(2):
            hop(way, 0, len(legs) - 1).start()
        share_out(0)

        def relay(s):
            ways = [way for way in range(2) if way == 0 or s < chain]
            for leg in range(len(legs)):
                for way in ways:
                    hop(way, s - 1, leg).wait_recv()
                    if s < chain - way:
                        hop(way, s, leg).start()
            if s < chain:
                share_out(s)

        def shared(first, last):
            for s in range(first, last):
                for item in range(3):
                    for way in range(2):
                        share(way, s, item).wait_recv()

        def pick(h):
            base = h * per_chunk
            e_lane = lax.broadcasted_iota(jnp.int32, (per_chunk, experts), 1)
            q = lax.broadcasted_iota(jnp.int32, (per_chunk, 1), 0)
            wide = lax.broadcasted_iota(jnp.int32, (per_chunk, per_chunk * tok_rows), 1)
            for cap in range(CAP):
                idx_all = bmeta[base : base + per_chunk, cap, :]
                w_all = bmeta[base : base + per_chunk, CAP + cap, :]
                for i in range(n_exp):
                    mine = e_lane == z * n_exp + i
                    idx = jnp.sum(jnp.where(mine, idx_all, 0.0), axis=1, keepdims=True)
                    w = jnp.sum(jnp.where(mine, w_all, 0.0), axis=1, keepdims=True)
                    idx = idx.astype(jnp.int32)
                    target = jnp.where(idx >= 0, q * tok_rows + idx, -1)
                    at = i * rows + cap * per_chunk
                    sel_s[h, at : at + per_chunk, :] = (wide == target).astype(F32).astype(BF16)
                    sel_w[h, at : at + per_chunk, :] = jnp.broadcast_to(w, (per_chunk, 128))
            s = sel_s[h]
            near = s_odd[...]
            evens = 2 * quarter
            s = s[:, : evens * tok_rows]
            x, g = [
                mm(s, bufs[item][h * evens : (h + 1) * evens].reshape(evens * tok_rows, feat))
                + mm(near, odd_rows[item, h].reshape(evens * SHARED, feat))
                for item in range(2)
            ]
            g = g * sel_w[h][:, 0:1]
            for i in range(n_exp):
                sel[h, i, 0] = x[i * rows : (i + 1) * rows].astype(BF16)
                sel[h, i, 1] = g[i * rows : (i + 1) * rows].astype(BF16)

        def y_copy(h, d):
            dc, dl = deltas[d]
            cc, ll, who = mate(dc, dl)
            return pltpu.make_async_remote_copy(
                src_ref=sel.at[h, cc * 2 + ll // 2],
                dst_ref=xg.at[h, slot],
                send_sem=y_send.at[h],
                recv_sem=y_recv.at[h, d],
                device_id=who,
                device_id_type=MESH,
            )

        def y_arrival(h, d):
            dc, dl = deltas[d]
            cc, ll, who = mate(2 - dc, n_local - dl)
            return pltpu.make_async_remote_copy(
                src_ref=sel.at[h, 0],
                dst_ref=xg.at[h, cc * n_local + ll],
                send_sem=y_send.at[h],
                recv_sem=y_recv.at[h, d],
                device_id=who,
                device_id_type=MESH,
            )

        def y_out(h):
            for d in range(len(deltas)):
                y_copy(h, d).start()
            pltpu.make_async_copy(sel.at[h, c * 2 + l // 2], xg.at[h, slot], own_sem.at[h]).start()

        def x_copy(h, dj):
            jj, who = peer(dj)
            return pltpu.make_async_remote_copy(
                src_ref=parts.at[h, jj],
                dst_ref=got.at[h, dj - 1],
                send_sem=x_send.at[h],
                recv_sem=x_recv.at[h, dj - 1],
                device_id=who,
                device_id_type=MESH,
            )

        def first_matmuls(h):
            for d in range(len(deltas)):
                y_arrival(h, d).wait_recv()
            pltpu.make_async_copy(sel.at[h, c * 2 + l // 2], xg.at[h, slot], own_sem.at[h]).wait()
            x = xg[h, :, 0].reshape(all_rows, feat)
            g = xg[h, :, 1].reshape(all_rows, feat)
            parts[h, :, 0] = mm(x, wg[...]).astype(BF16).reshape(n_tp, strip, half)
            parts[h, :, 1] = mm(x, wu[...]).astype(BF16).reshape(n_tp, strip, half)
            parts[h, :, 2] = mm(g, wd[...], LAST).astype(BF16).reshape(n_tp, strip, half)
            for dj in range(1, n_tp):
                x_copy(h, dj).start()

        def a_copy(h, dj, arrival=False):
            jj, who = peer(dj)
            at = lax.rem(j + n_tp - dj, n_tp) if arrival else j
            return pltpu.make_async_remote_copy(
                src_ref=acts.at[h, j],
                dst_ref=acts.at[h, at],
                send_sem=a_send.at[h],
                recv_sem=a_recv.at[h, dj - 1],
                device_id=who,
                device_id_type=MESH,
            )

        def activation(h):
            for dj in range(1, n_tp):
                x_copy(h, dj).wait_recv()
            total = []
            for kind in range(3):
                value = parts[h, j, kind].astype(F32)
                for dj in range(1, n_tp):
                    value = value + got[h, dj - 1, kind].astype(F32)
                total.append(value)
            gate, up_val, d_hidden = total
            sig = jax.nn.sigmoid(gate)
            act = gate * sig
            acts[h, j, 0] = (act * up_val).astype(BF16)
            acts[h, j, 1] = (d_hidden * up_val * sig * (1.0 + gate * (1.0 - sig))).astype(BF16)
            acts[h, j, 2] = (d_hidden * act).astype(BF16)
            for dj in range(1, n_tp):
                a_copy(h, dj).start()

        def o_copy(h, d):
            dc, dl = deltas[d]
            cc, ll, who = mate(dc, dl)
            return pltpu.make_async_remote_copy(
                src_ref=ob.at[h, cc * n_local + ll],
                dst_ref=rob.at[h, slot],
                send_sem=o_send.at[h],
                recv_sem=o_recv.at[h, d],
                device_id=who,
                device_id_type=MESH,
            )

        def o_arrival(h, d):
            dc, dl = deltas[d]
            cc, ll, who = mate(2 - dc, n_local - dl)
            return pltpu.make_async_remote_copy(
                src_ref=ob.at[h, 0],
                dst_ref=rob.at[h, cc * n_local + ll],
                send_sem=o_send.at[h],
                recv_sem=o_recv.at[h, d],
                device_id=who,
                device_id_type=MESH,
            )

        def own_out(h):
            return pltpu.make_async_copy(ob.at[h, slot], rob.at[h, slot], own_sem.at[CHUNKS + h])

        def last_matmuls(h):
            for dj in range(1, n_tp):
                a_copy(h, dj, True).wait_recv()
            hidden = acts[h, :, 0].reshape(all_rows, half)
            d_gate = acts[h, :, 1].reshape(all_rows, half)
            d_up = acts[h, :, 2].reshape(all_rows, half)
            ob[h, :, 0] = mm(hidden, wd[...]).astype(BF16).reshape(plane, rows, feat)
            back = mm(d_gate, wg[...], LAST) + mm(d_up, wu[...], LAST)
            ob[h, :, 1] = back.astype(BF16).reshape(plane, rows, feat)
            for d in range(len(deltas)):
                o_copy(h, d).start()
            own_out(h).start()

        def weight_grads(h):
            x = xg[h, :, 0].reshape(all_rows, feat)
            g = xg[h, :, 1].reshape(all_rows, feat)
            hidden = acts[h, :, 0].reshape(all_rows, half)
            d_gate = acts[h, :, 1].reshape(all_rows, half)
            d_up = acts[h, :, 2].reshape(all_rows, half)
            for acc, out, a, b in (
                (acc_d, o_d, hidden, g),
                (acc_g, o_g, x, d_gate),
                (acc_u, o_u, x, d_up),
            ):
                value = mm(a, b, FIRST)
                if h > 0:
                    value = acc[...] + value
                if h < CHUNKS - 1:
                    acc[...] = value
                else:
                    out[...] = value.astype(BF16)

        def contributions(h):
            for d in range(len(deltas)):
                o_arrival(h, d).wait_recv()
            own_out(h).wait()
            base = h * per_chunk
            s = sel_s[h]
            outs, backs = [], []
            for i in range(n_exp):
                for kind, keep in ((0, outs), (1, backs)):
                    value = rob[h, 2 * i, kind].astype(F32) + rob[h, 2 * i + 1, kind].astype(F32)
                    keep.append(value.astype(BF16))
            row_out = jnp.concatenate(outs, axis=0).astype(F32) * sel_w[h][:, 0:1]
            high = row_out.astype(BF16)
            low = (row_out - high.astype(F32)).astype(BF16)
            mix = mm(s, high, FIRST) + mm(s, low, FIRST)
            c_mix[base : base + per_chunk] = mix.reshape(per_chunk, tok_rows, feat)
            back = mm(s, jnp.concatenate(backs, axis=0), FIRST)
            c_back[base : base + per_chunk] = back.reshape(per_chunk, tok_rows, feat)

        def gathered(h):
            shared(quarter * h, quarter * (h + 1))
            pick(h)
            y_out(h)

        pieces = (
            (c_mix, s_mix, r_mix, t_mix, n_mix),
            (c_back, s_back, r_back, t_back, n_back),
        )

        def lend(way, a, item):
            _, _, _, send, receive = pieces[item]
            return pltpu.make_async_remote_copy(
                src_ref=send.at[way, a],
                dst_ref=receive.at[way, a],
                send_sem=ln_send.at[item],
                recv_sem=ln_recv.at[way, a, item],
                device_id=one[way],
                device_id_type=MESH,
            )

        def fold(way, s, item, part):
            _, send, receive, _, _ = pieces[item]
            return pltpu.make_async_remote_copy(
                src_ref=cut(send.at[way, s], part),
                dst_ref=cut(receive.at[way, s], part),
                send_sem=rs_send.at[item],
                recv_sem=rs_recv.at[way, s, item, part],
                device_id=two[way],
                device_id_type=MESH,
            )

        def lend_out(way, a, item):
            contrib, _, _, send, _ = pieces[item]
            send[way, a] = contrib[odd(1 - way, a)].astype(BF16)
            lend(way, a, item).start()

        def add_on(way, away, item):
            contrib, send, receive, _, lent = pieces[item]
            s = chain - away
            if away < chain:
                lend(way, away, item).wait_recv()
            for part in range(PARTS):
                at = pl.ds(part * piece, piece)
                value = contrib[even(2 * away - way), at]
                if away < chain:
                    value = value + lent[way, away, at].astype(F32)
                if away < chain - 1 + way:
                    fold(way, s - 1, item, part).wait_recv()
                    value = value + receive[way, s - 1, at].astype(F32)
                send[way, s, at] = value.astype(BF16)
                fold(way, s, item, part).start()

        def returned(h):
            contributions(h)
            if h == CHUNKS - 1:
                for item in range(2):
                    add_on(1, chain, item)
            for a in range(quarter * (h + 1) - 1, quarter * h - 1, -1):
                for item in range(2):
                    for way in range(2):
                        lend_out(way, a, item)

        for s in range(1, chain + 1):
            relay(s)
            if s == 2:
                gathered(0)
            if s == 4:
                gathered(1)
                for load in loads:
                    load.wait()
                first_matmuls(0)
            if s == 6:
                gathered(2)
                activation(0)
                first_matmuls(1)
        gathered(3)
        first_matmuls(2)
        activation(1)
        last_matmuls(0)
        first_matmuls(3)
        activation(2)
        last_matmuls(1)
        weight_grads(0)
        activation(3)
        returned(0)
        last_matmuls(2)
        weight_grads(1)
        returned(1)
        last_matmuls(3)
        weight_grads(2)
        weight_grads(3)
        stores = [
            pltpu.make_async_copy(src, dst.at[0], w_sem.at[3 + i])
            for i, (src, dst) in enumerate(((o_g, gg_ref), (o_u, gu_ref), (o_d, gd_ref)))
        ]
        for store in stores:
            store.start()
        returned(2)
        returned(3)

        for a in range(chain - 1, 0, -1):
            for item in range(2):
                for way in range(2):
                    add_on(way, a, item)

        def sent(ref, sem):
            pltpu.make_async_remote_copy(
                src_ref=ref, dst_ref=ref, send_sem=sem, recv_sem=own_sem.at[0],
                device_id=two[0], device_id_type=MESH,
            ).wait_send()

        for h in range(CHUNKS):
            sent(xg.at[h, pl.ds(0, plane - 1)], y_send.at[h])
            sent(ob.at[h, pl.ds(0, plane - 1)], o_send.at[h])
            sent(parts.at[h, pl.ds(0, n_tp - 1)], x_send.at[h])
            sent(acts.at[h, pl.ds(0, n_tp - 1)], a_send.at[h])
        for item in range(2):
            sent(bufs[item].at[pl.ds(0, 2 * chain - 1)], ag_send.at[item])
            sent(lent_rows.at[item], sh_send.at[item])
            sent(pieces[item][3], ln_send.at[item])
        sent(bmeta.at[pl.ds(0, 2 * chain - 1)], ag_send.at[2])
        sent(bmeta.at[pl.ds(0, 2 * chain)], sh_send.at[2])
        for item, out in ((0, o_mix), (1, o_back)):
            contrib, _, receive, _, lent = pieces[item]
            value = contrib[0]
            for way in range(2):
                lend(way, 0, item).wait_recv()
                value = value + lent[way, 0].astype(F32)
                for part in range(PARTS):
                    fold(way, chain - 1, item, part).wait_recv()
                value = value + receive[way, chain - 1].astype(F32)
            out[...] = value.astype(BF16)
        stores += [
            pltpu.make_async_copy(o_mix, mixed_ref, w_sem.at[6]),
            pltpu.make_async_copy(o_back, gtok_ref, w_sem.at[7]),
        ]
        for store in stores[3:]:
            store.start()

        for item in range(2):
            sent(bufs[item].at[pl.ds(0, 2 * chain - 1)], rs_send.at[item])
        for store in stores:
            store.wait()

    scratch = [
        pltpu.VMEM((feat, half), BF16),
        pltpu.VMEM((feat, half), BF16),
        pltpu.VMEM((half, feat), BF16),
        pltpu.VMEM((2 * chain, tok_rows, feat), BF16),
        pltpu.VMEM((2 * chain, tok_rows, feat), BF16),
        pltpu.VMEM((ring, 8, experts), F32),
        pltpu.VMEM((CHUNKS, n_exp * rows, per_chunk * tok_rows), BF16),
        pltpu.VMEM((CHUNKS, n_exp * rows, 128), F32),
        pltpu.VMEM((CHUNKS, n_exp, 2, rows, feat), BF16),
        pltpu.VMEM((CHUNKS, plane, 2, rows, feat), BF16),
        pltpu.VMEM((CHUNKS, n_tp, 3, strip, half), BF16),
        pltpu.VMEM((CHUNKS, n_tp - 1, 3, strip, half), BF16),
        pltpu.VMEM((CHUNKS, n_tp, 3, strip, half), BF16),
        pltpu.VMEM((feat, half), F32),
        pltpu.VMEM((feat, half), F32),
        pltpu.VMEM((half, feat), F32),
        pltpu.VMEM((CHUNKS, plane, 2, rows, feat), BF16),
        pltpu.VMEM((CHUNKS, plane, 2, rows, feat), BF16),
        pltpu.VMEM((ring, tok_rows, feat), F32),
        pltpu.VMEM((ring, tok_rows, feat), F32),
        *[pltpu.VMEM((2, chain, tok_rows, feat), BF16)] * 8,
        pltpu.VMEM((tok_rows, feat), BF16),
        pltpu.VMEM((tok_rows, feat), BF16),
        pltpu.VMEM((feat, half), BF16),
        pltpu.VMEM((feat, half), BF16),
        pltpu.VMEM((half, feat), BF16),
        pltpu.SemaphoreType.DMA((8,)),
        pltpu.SemaphoreType.DMA((3,)),
        pltpu.SemaphoreType.DMA((2, chain, len(legs))),
        pltpu.SemaphoreType.DMA((CHUNKS,)),
        pltpu.SemaphoreType.DMA((CHUNKS, plane - 1)),
        pltpu.SemaphoreType.DMA((CHUNKS,)),
        pltpu.SemaphoreType.DMA((CHUNKS, n_tp - 1)),
        pltpu.SemaphoreType.DMA((CHUNKS,)),
        pltpu.SemaphoreType.DMA((CHUNKS, n_tp - 1)),
        pltpu.SemaphoreType.DMA((CHUNKS,)),
        pltpu.SemaphoreType.DMA((CHUNKS, plane - 1)),
        pltpu.SemaphoreType.DMA((2,)),
        pltpu.SemaphoreType.DMA((2, chain, 2, PARTS)),
        pltpu.SemaphoreType.DMA((2 * CHUNKS,)),
        pltpu.VMEM((n_exp * rows, 2 * quarter * SHARED), BF16),
        pltpu.VMEM((2, 2, chain, SHARED, feat), BF16),
        pltpu.VMEM((2, CHUNKS, 2 * quarter, SHARED, feat), BF16),
        pltpu.SemaphoreType.DMA((3,)),
        pltpu.SemaphoreType.DMA((2, chain, 3)),
        pltpu.SemaphoreType.DMA((2,)),
        pltpu.SemaphoreType.DMA((2, chain, 2)),
    ]
    return kernel, scratch


def deliver(arrays):
    count = len(arrays)

    def kernel(*refs):
        sources, targets, held = refs[:count], refs[count : 2 * count], refs[2 * count : 3 * count]
        in_sem, out_sem = refs[3 * count :]
        loads = [pltpu.make_async_copy(sources[i], held[i], in_sem.at[i]) for i in range(count)]
        stores = [pltpu.make_async_copy(held[i], targets[i], out_sem.at[i]) for i in range(count)]
        for load in loads:
            load.start()
        for load, store in zip(loads, stores):
            load.wait()
            store.start()
        for store in stores:
            store.wait()

    anywhere = pl.BlockSpec(memory_space=pl.ANY)
    return pl.pallas_call(
        kernel,
        out_shape=tuple(jax.ShapeDtypeStruct(a.shape, a.dtype) for a in arrays),
        in_specs=[anywhere] * count,
        out_specs=(anywhere,) * count,
        scratch_shapes=[pltpu.VMEM(a.shape, a.dtype) for a in arrays]
        + [pltpu.SemaphoreType.DMA((count,))] * 2,
        name="deliver",
    )(*arrays)


def solution(mesh):
    ring, n_local, n_tp = mesh.shape["node"] // 2, mesh.shape["local"], mesh.shape["tp"]

    def shards(tokens, grad_out, routes, route_weight, w_gate, w_up, w_down):
        tok_rows, feat = tokens.shape
        half = w_gate.shape[2]
        kernel, scratch = make_kernel(ring, n_local, n_tp, tok_rows, routes.shape[1], feat, half)
        vmem = pl.BlockSpec(memory_space=pltpu.VMEM)
        outs = pl.pallas_call(
            kernel,
            out_shape=(
                jax.ShapeDtypeStruct((tok_rows, feat), BF16),
                jax.ShapeDtypeStruct((tok_rows, feat), BF16),
                jax.ShapeDtypeStruct((1, feat, half), BF16),
                jax.ShapeDtypeStruct((1, feat, half), BF16),
                jax.ShapeDtypeStruct((1, half, feat), BF16),
            ),
            in_specs=[vmem] * 4 + [pl.BlockSpec(memory_space=pl.ANY)] * 3,
            out_specs=(pl.BlockSpec(memory_space=pl.ANY),) * 5,
            scratch_shapes=scratch,
            compiler_params=pltpu.CompilerParams(collective_id=0, has_side_effects=True),
            name="routed_experts",
        )(tokens, grad_out, routes.T, route_weight.T, w_gate, w_up, w_down)
        return deliver(outs)

    return jax.shard_map(
        shards,
        mesh=mesh,
        in_specs=(
            P(("node", "local"), "tp"),
            P(("node", "local"), "tp"),
            P(("node", "local"), None),
            P(("node", "local"), None),
            P(("node", "local"), "tp", None),
            P(("node", "local"), "tp", None),
            P(("node", "local"), None, "tp"),
        ),
        out_specs=(
            P(("node", "local"), "tp"),
            P(("node", "local"), "tp"),
            P(("node", "local"), "tp", None),
            P(("node", "local"), "tp", None),
            P(("node", "local"), None, "tp"),
        ),
        check_vma=False,
    )
```
